512 devices in a mesh: dp: 8 (over y), tm: 64 (over x, z, core).
Axes of the slice: x: 4, y: 8, z: 8, core: 2. Of those that a mesh axis runs over, the one named last changes fastest.
Arguments:
- signal: bfloat16 [8, 8192, 512], P('dp', 'tm'), may hold values from -16 to 16
- conv_weight: bfloat16 [2, 1024, 512], replicated, may hold values from -0.1875 to 0.1875
- res_weight: bfloat16 [2, 256, 768], replicated, may hold values from -0.375 to 0.375
- grad_out: bfloat16 [8, 8192, 512], P('dp', 'tm'), may hold values from -6 to 6
- skip_cotangent: bfloat16 [8, 8192, 256], P('dp', 'tm'), may hold values from -16 to 16
Outputs:
- input_grad: bfloat16 [8, 8192, 512], P('dp', 'tm')
- conv_grad: bfloat16 [2, 1024, 512], P(None, 'tm')
- res_grad: bfloat16 [2, 256, 768], replicated
The draws below stay inside these ranges and needn't reach their ends.
All inputs are finite; a program needn't handle non-finite values.
Results may differ from the reference program's by a relative error of at most 0.0063.
Values may be sent and summed in bfloat16 or wider, within the bound.
A program may use at most 64 MiB of HBM per device.

```python
import jax
import jax.numpy as jnp
from jax import lax

C = 512
GC = 256
SK = 256
STREAMS = 8
TIME = 8192
DILATION_INNER = 32
DILATION_OUTER = 1024


def raised(drawn, key, source, target, parts, factor):
    def block_of(position):
        return (jnp.arange(drawn.shape[position]) // (drawn.shape[position] // parts)).reshape((-1,) + (1,) * (drawn.ndim - 1 - position))

    near = jax.random.permutation(key, parts)[block_of(target)]
    other_side = (block_of(target) + parts // 2) % parts
    return jnp.where((block_of(source) == near) | (block_of(source) == other_side), factor * drawn, drawn)


def steps_of(stream_key, dims, pieces, least, top_value):
    def one(position, blocks):
        draws = jax.random.uniform(jax.random.fold_in(jax.random.fold_in(stream_key, 6), position), (blocks,), jnp.float32, least / len(pieces), top_value / len(pieces))
        return jnp.repeat(jnp.exp(draws), dims[position] // blocks).reshape((-1,) + (1,) * (len(dims) - position - 1))

    level = one(*pieces[0])
    for cut in pieces[1:]:
        level = level * one(*cut)
    return level


def noise(key, dims, scale, reach, split=(), kind=jnp.bfloat16):
    entries = jax.random.normal(key, dims, jnp.float32) * scale
    if len(split) > 0:
        entries = steps_of(key, dims, split, -0.22, 0.18) * entries
    return jnp.clip(entries, min=-reach, max=reach).astype(kind)


def bell_draw_with(rng, shape, scale, bound, shards, heavy, held_as=jnp.bfloat16):
    entries = scale * jax.random.normal(rng, shape, jnp.float32)
    if shards:
        entries = entries * steps_of(rng, shape, shards, -0.22, 0.18)
    return jnp.clip(raised(entries, jax.random.fold_in(rng, 3), *heavy), -bound, bound).astype(held_as)


def setup_inputs(seed: int = 0) -> dict:
    key_of = jax.random.split(jax.random.key(seed), 6)
    return {
        "signal": bell_draw_with(key_of[0], (STREAMS, TIME, C), 1.0, 16.0, ((0, 8), (1, 64)), (1, 2, 64, 4.0)),
        "conv_weight": noise(key_of[1], (2, 2 * C, 2 * GC), (2 * C) ** -0.5, 0.1875),
        "res_weight": noise(key_of[2], (2, GC, C + SK), GC ** -0.5, 0.375),
        "grad_out": noise(key_of[3], (STREAMS, TIME, C), 1.0, 6.0, ((0, 8), (1, 64))),
        "skip_cotangent": bell_draw_with(key_of[4], (STREAMS, TIME, SK), 1.0, 16.0, ((0, 8), (1, 64)), (1, 2, 64, 4.0)),
    }


def delay(x, dist):
    zeros = jnp.zeros((dist, x.shape[1]), x.dtype)
    return jnp.concatenate([zeros, x[:-dist]], axis=0)


def shift_forward(x, dist):
    zeros = jnp.zeros((dist, x.shape[1]), x.dtype)
    return jnp.concatenate([x[dist:], zeros], axis=0)


def one_stream(signal, conv_weight, res_weight, grad_out, skip_cotangent):
    tap_distances = (DILATION_INNER, DILATION_OUTER)
    x = signal
    cats = []
    zvals = []
    hvals = []
    for layer in range(2):
        past = delay(x, tap_distances[layer])
        cat = jnp.concatenate([past, x], axis=1)
        z = jnp.dot(cat, conv_weight[layer], preferred_element_type=jnp.float32)
        h = (jnp.tanh(z[:, :GC]) * jax.nn.sigmoid(z[:, GC:])).astype(jnp.bfloat16)
        cats.append(cat)
        zvals.append(z)
        hvals.append(h)
        if layer == 0:
            resid = jnp.dot(h, res_weight[0][:, :C], preferred_element_type=jnp.float32)
            x = (x.astype(jnp.float32) + resid).astype(jnp.bfloat16)
    grad = grad_out.astype(jnp.float32)
    conv_terms = [None, None]
    res_terms = [None, None]
    for layer in (1, 0):
        outer = jnp.concatenate([grad.astype(jnp.bfloat16), skip_cotangent], axis=1)
        dh = lax.dot_general(outer, res_weight[layer], (((1,), (1,)), ((), ())), preferred_element_type=jnp.float32)
        z = zvals[layer]
        tf = jnp.tanh(z[:, :GC])
        sg = jax.nn.sigmoid(z[:, GC:])
        dz = jnp.concatenate([dh * sg * (1.0 - tf * tf), dh * tf * sg * (1.0 - sg)], axis=1).astype(jnp.bfloat16)
        wcat = lax.dot_general(dz, conv_weight[layer], (((1,), (1,)), ((), ())), preferred_element_type=jnp.float32)
        dpast = wcat[:, :C].astype(jnp.bfloat16)
        grad = grad + wcat[:, C:] + shift_forward(dpast, tap_distances[layer]).astype(jnp.float32)
        conv_terms[layer] = lax.dot_general(cats[layer], dz, (((0,), (0,)), ((), ())), preferred_element_type=jnp.float32)
        res_terms[layer] = lax.dot_general(hvals[layer], outer, (((0,), (0,)), ((), ())), preferred_element_type=jnp.float32)
    return grad.astype(jnp.bfloat16), jnp.stack(conv_terms), jnp.stack(res_terms)


def reference(signal, conv_weight, res_weight, grad_out, skip_cotangent):
    def step(carry, items):
        conv_sum, res_sum = carry
        sig, gout, sgrad = items
        igrad, conv_t, res_t = one_stream(sig, conv_weight, res_weight, gout, sgrad)
        return (conv_sum + conv_t, res_sum + res_t), igrad

    start = (jnp.zeros((2, 2 * C, 2 * GC), jnp.float32), jnp.zeros((2, GC, C + SK), jnp.float32))
    (conv_sum, res_sum), input_grad = lax.scan(step, start, (signal, grad_out, skip_cotangent))
    factor = float(STREAMS * TIME) ** -0.5
    conv_grad = (conv_sum * factor).astype(jnp.bfloat16)
    res_grad = (res_sum * factor).astype(jnp.bfloat16)
    return input_grad, conv_grad, res_grad
```

```python
import functools

import jax
import jax.numpy as jnp
from jax import lax
from jax.experimental import pallas as pl
from jax.experimental.pallas import tpu as pltpu
from jax.sharding import Mesh
from jax.sharding import PartitionSpec as P

TM = ("tm_0", "tm_1", "tm_2")
NX, NZ, NC = 4, 8, 2
MESH = pl.DeviceIdType.MESH
BF = jnp.bfloat16
F32 = jnp.float32


def mm(a, b):
    return jnp.dot(a, b, preferred_element_type=F32)


def mm_t(a, b):
    return lax.dot_general(a, b, (((1,), (1,)), ((), ())), preferred_element_type=F32)


def t_mm(a, b):
    return lax.dot_general(a, b, (((0,), (0,)), ((), ())), preferred_element_type=F32)


class Links:
    def __init__(self, send, recv, local):
        self.send, self.recv, self.local = send, recv, local
        self.n_remote = self.n_local = 0
        self.sent = []
        self.stored = []

    def push(self, src, dst, device):
        i = self.n_remote
        self.n_remote += 1
        copy = pltpu.make_async_remote_copy(
            src_ref=src,
            dst_ref=dst,
            send_sem=self.send.at[i],
            recv_sem=self.recv.at[i],
            device_id=device,
            device_id_type=MESH,
        )
        copy.start()
        self.sent.append(copy)
        return copy

    def move(self, src, dst, last=False):
        i = self.n_local
        self.n_local += 1
        copy = pltpu.make_async_copy(src, dst, self.local.at[i])
        copy.start()
        if last:
            self.stored.append(copy)
        return copy

    def finish(self):
        for copy in self.sent:
            copy.wait_send()
        for copy in self.stored:
            copy.wait()


def kernel(
    ny, factor,
    sig, cw, rw, go_in, sk_in,
    ig_out, cg_out, rg_out,
    x0, p0, w, r, go, sk, xh, ph, tf0, sg0, hk, hs, dz1, dz1s, dz0, dz0s,
    gp, gpb, dp, dpr, dp0, dp0r, igv,
    cs1, cx1, cz1, czr1, cy1, cyr1,
    cs0, cx0, cz0, czr0, cy0, cyr0, cgv,
    rs, rxr, rz, rzr, ry, ryr, rg, rx, rc,
    send, recv, local,
):
    y = lax.axis_index("dp")
    x = lax.axis_index("tm_0")
    z = lax.axis_index("tm_1")
    c = lax.axis_index("tm_2")
    t = x * (NZ * NC) + z * NC + c
    nt = NX * NZ * NC
    near = 32
    far = 8
    rows, width = 128, 512
    gated = 256

    def at(dy=0, dx=0, dz=0, dc=0):
        return (
            lax.rem(y + dy, ny), lax.rem(x + dx, NX), lax.rem(z + dz, NZ), lax.rem(c + dc, NC)
        )

    def along(d):
        s = lax.rem(t + (d + nt), nt)
        return (y, s // (NZ * NC), lax.rem(s // NC, NZ), lax.rem(s, NC))

    partner = at(dc=1)
    xs = [at(dx=d) for d in range(1, NX)]
    zs = [at(dz=d) for d in range(1, NZ)]
    ys = [at(dy=d) for d in range(1, ny)]
    yc = [(dy, dc) for dy in range(ny) for dc in range(NC) if dy or dc]

    barrier = pltpu.get_barrier_semaphore()
    greeted = [along(1), along(-1), along(far), along(-far)]
    greeted += xs + zs + [at(dy=dy, dc=dc) for dy, dc in yc]
    for device in greeted:
        pl.semaphore_signal(barrier, inc=1, device_id=device, device_id_type=MESH)

    link = Links(send, recv, local)
    own, other = pl.ds(0, rows), pl.ds(rows, rows)
    in_x = link.move(sig.at[0], x0.at[own])
    in_p = link.move(sig.at[0, pl.ds(0, rows - near)], p0.at[pl.ds(near, rows - near)])
    in_w0 = link.move(cw.at[0], w.at[0])
    in_r0 = link.move(rw.at[0], r.at[0])
    in_go = link.move(go_in.at[0], go.at[own])
    in_sk = link.move(sk_in.at[0], sk.at[own])
    in_r1 = link.move(rw.at[1], r.at[1])
    in_w1 = link.move(cw.at[1], w.at[1])

    def layer0(lo, n):
        part = pl.ds(lo, n)
        zv = mm(p0[part, :], w[0, 0:width, :]) + mm(x0[part, :], w[0, width : 2 * width, :])
        tf = jnp.tanh(zv[:, :gated])
        sg = jax.nn.sigmoid(zv[:, gated:])
        h = (tf * sg).astype(BF)
        tf0[part, :] = tf
        sg0[part, :] = sg
        xh[part, width : width + gated] = h
        xh[part, 0:width] = (x0[part, :].astype(F32) + mm(h, r[0, :, 0:width])).astype(BF)

    in_x.wait()
    in_p.wait()
    in_w0.wait()
    in_r0.wait()
    layer0(near, rows - near)
    in_go.wait()
    in_sk.wait()

    pl.semaphore_wait(barrier, len(greeted))
    halo = link.push(x0.at[pl.ds(rows - near, near)], p0.at[pl.ds(0, near)], along(1))
    high = pl.ds(near, rows - near)
    low = pl.ds(0, near)
    far_high = link.push(xh.at[high], ph.at[high], along(far))
    x0_there = link.push(x0.at[own], x0.at[other], partner)
    go_there = link.push(go.at[own], go.at[other], partner)
    sk_there = link.push(sk.at[own], sk.at[other], partner)

    in_r1.wait()
    e1 = mm_t(go[own, :], r[1, :, 0:width]) + mm_t(sk[own, :], r[1, :, width:])
    es0 = mm_t(sk[own, :], r[0, :, width:])

    halo.wait_recv()
    p0[low, :] = jnp.where(t == 0, jnp.zeros((near, width), BF), p0[low, :])
    layer0(0, near)
    far_low = link.push(xh.at[low], ph.at[low], along(far))
    p0_there = link.push(p0.at[own], p0.at[other], partner)
    x1_there = link.push(xh.at[own, pl.ds(0, width)], xh.at[other, pl.ds(0, width)], partner)
    in_w1.wait()
    zc1 = mm(xh[own, 0:width], w[1, width : 2 * width, :])

    far_high.wait_recv()
    far_low.wait_recv()
    ph[own, :] = jnp.where(t < far, jnp.zeros((rows, width + gated), BF), ph[own, :])
    z1 = zc1 + mm(ph[own, 0:width], w[1, 0:width, :])
    tf = jnp.tanh(z1[:, :gated])
    sg = jax.nn.sigmoid(z1[:, gated:])
    h1 = (tf * sg).astype(BF)
    dza = (e1 * sg * (1.0 - tf * tf)).astype(BF)
    dzb = (e1 * tf * sg * (1.0 - sg)).astype(BF)
    dpast = (mm_t(dza, w[1, 0:width, 0:gated]) + mm_t(dzb, w[1, 0:width, gated:])).astype(BF)
    dp[own, :] = dpast
    back = link.push(dp.at[own], dpr, along(-far))
    first = c == 0
    dz1[own, :] = jnp.where(first, dza, dzb)
    dz1s[...] = jnp.where(first, dzb, dza)
    dz1_there = link.push(dz1s, dz1.at[other], partner)
    half = gated // 2
    for i, hv in enumerate((h1, xh[own, width:], ph[own, width:])):
        lo, hi = hv[:, :half], hv[:, half:]
        hk[i, own, :] = jnp.where(first, lo, hi)
        hs[i] = jnp.where(first, hi, lo)
    hk_there = link.push(hs, hk.at[:, other, :], partner)
    dp_there = link.push(dp.at[own], dp.at[other], partner)
    p1_there = link.push(ph.at[own, pl.ds(0, width)], ph.at[other, pl.ds(0, width)], partner)
    gpv = go[own, :].astype(F32) + (
        mm_t(dza, w[1, width : 2 * width, 0:gated]) + mm_t(dzb, w[1, width : 2 * width, gated:])
    )
    gp[...] = gpv
    gpb[own, :] = gpv.astype(BF)
    gpb_there = link.push(gpb.at[own], gpb.at[other], partner)

    go_there.wait_recv()
    sk_there.wait_recv()
    hk_there.wait_recv()
    dp_there.wait_recv()
    res1a = t_mm(hk[0], go[...])
    res1b = t_mm(hk[0], sk[...])
    res0b = t_mm(hk[1], sk[...])
    gpb_there.wait_recv()
    res0a = t_mm(hk[1], gpb[...]) + t_mm(hk[2], dp[...])
    cut = 384
    for i, (a, b) in enumerate(((res0a, res0b), (res1a, res1b))):
        rs[2 * i] = a[:, :cut].astype(BF)
        rs[2 * i + 1, :, 0 : width - cut] = a[:, cut:].astype(BF)
        rs[2 * i + 1, :, width - cut :] = b.astype(BF)

    def to_x(src, dst):
        return [
            link.push(src.at[lax.rem(x + d, NX)], dst.at[d - 1], xs[d - 1]) for d in range(1, NX)
        ]

    def to_z(src, dst):
        return [
            link.push(src.at[lax.rem(z + d, NZ)], dst.at[d - 1], zs[d - 1]) for d in range(1, NZ)
        ]

    def summed(copies, own_part, slots):
        total = own_part.astype(F32)
        for i, copy in enumerate(copies):
            copy.wait_recv()
            total = total + slots[i].astype(F32)
        return total

    def conv_parts(past, cur, dz, out):
        dzv = dz[...]
        for i in range(NX):
            src = past if i < 2 else cur
            col = (i % 2) * 256
            out[i] = t_mm(src[:, col : col + 256], dzv).astype(BF)

    res_x = to_x(rs, rxr)
    dz1_there.wait_recv()
    x1_there.wait_recv()
    p1_there.wait_recv()
    conv_parts(ph, xh, dz1, cs1)
    conv1_x = to_x(cs1, cx1)

    back.wait_recv()
    g1 = gp[...] + jnp.where(t < nt - far, dpr[...].astype(F32), 0.0)
    e0 = mm_t(g1.astype(BF), r[0, :, 0:width]) + es0
    tf = tf0[...]
    sg = sg0[...]
    dza = (e0 * sg * (1.0 - tf * tf)).astype(BF)
    dzb = (e0 * tf * sg * (1.0 - sg)).astype(BF)
    dz0[own, :] = jnp.where(first, dza, dzb)
    dz0s[...] = jnp.where(first, dzb, dza)
    dz0_there = link.push(dz0s, dz0.at[other], partner)
    dpast = (mm_t(dza, w[0, 0:width, 0:gated]) + mm_t(dzb, w[0, 0:width, gated:])).astype(BF)
    dp0[...] = dpast
    halo_back = link.push(dp0.at[low], dp0r, along(-1))

    rzv = summed(res_x, rs[x], rxr).astype(BF)
    for k in range(NZ):
        rz[k] = rzv[16 * k : 16 * k + 16, :]
    res_z = to_z(rz, rzr)

    x0_there.wait_recv()
    p0_there.wait_recv()
    dz0_there.wait_recv()
    conv_parts(p0, x0, dz0, cs0)
    conv0_x = to_x(cs0, cx0)

    wc = mm_t(dza, w[0, width : 2 * width, 0:gated]) + mm_t(dzb, w[0, width : 2 * width, gated:])
    halo_back.wait_recv()
    tail = jnp.where(t < nt - 1, dp0r[...].astype(F32), 0.0)
    moved = jnp.concatenate([dp0[near:, :].astype(F32), tail], axis=0)
    igv[...] = (g1 + wc + moved).astype(BF)
    link.move(igv, ig_out.at[0], last=True)

    def conv_to_z(copies, parts, slots, out, out_slots):
        v = summed(copies, parts[x], slots).astype(BF)
        for k in range(NZ):
            out[k] = v[32 * k : 32 * k + 32, :]
        return to_z(out, out_slots)

    def conv_to_y(copies, parts, slots, out, out_slots):
        v = summed(copies, parts[z], slots).astype(BF)
        out[0] = v[:16, :]
        out[1] = v[16:, :]
        sends = []
        for i, (dy, dc) in enumerate(yc):
            sends.append(
                link.push(out.at[lax.rem(c + dc, NC)], out_slots.at[i], at(dy=dy, dc=dc))
            )
        return sends

    def conv_final(layer, copies, part, slots):
        mine = part[c].astype(F32)
        theirs = jnp.zeros((16, 256), F32)
        for i, (dy, dc) in enumerate(yc):
            copies[i].wait_recv()
            v = slots[i].astype(F32)
            if dc:
                theirs = theirs + v
            else:
                mine = mine + v
        cgv[layer, :, 0:256] = (jnp.where(first, mine, theirs) * factor).astype(BF)
        cgv[layer, :, 256:512] = (jnp.where(first, theirs, mine) * factor).astype(BF)

    conv1_z = conv_to_z(conv1_x, cs1, cx1, cz1, czr1)

    ryv = summed(res_z, rz[z], rzr).astype(BF)
    ry[...] = ryv
    res_y = [link.push(ry, ryr.at[d - 1], ys[d - 1]) for d in range(1, ny)]

    conv0_z = conv_to_z(conv0_x, cs0, cx0, cz0, czr0)
    conv1_y = conv_to_y(conv1_z, cz1, czr1, cy1, cyr1)

    rf = (summed(res_y, ryv, ryr) * factor).astype(BF)
    rg[z] = rf
    res_gz = [link.push(rg.at[z], rg.at[z], device) for device in zs]

    conv0_y = conv_to_y(conv0_z, cz0, czr0, cy0, cyr0)
    for copy in res_gz:
        copy.wait_recv()
    for k in range(NZ):
        rx[x, 16 * k : 16 * k + 16, :] = rg[k]
    res_gx = [link.push(rx.at[x], rx.at[x], device) for device in xs]

    conv_final(1, conv1_y, cy1, cyr1)
    conv_final(0, conv0_y, cy0, cyr0)
    link.move(cgv, cg_out, last=True)

    for copy in res_gx:
        copy.wait_recv()
    res_gc = link.push(rx, rc, partner)
    for i in range(NX):
        place = rg_out.at[i // 2, pl.ds(c * half, half), pl.ds((i % 2) * cut, cut)]
        link.move(rx.at[i], place, last=True)
    res_gc.wait_recv()
    for i in range(NX):
        place = rg_out.at[i // 2, pl.ds((1 - c) * half, half), pl.ds((i % 2) * cut, cut)]
        link.move(rc.at[i], place, last=True)
    link.finish()


def body(signal, conv_weight, res_weight, grad_out, skip_cotangent):
    ny = lax.axis_size("dp")
    total = signal.shape[0] * signal.shape[1] * ny * lax.axis_size(TM)
    factor = float(total) ** (-0.5)
    yc = ny * NC - 1

    def v(shape, dtype=BF):
        return pltpu.VMEM(shape, dtype)

    scratch = [
        v((256, 512)), v((256, 512)), v((2, 1024, 512)), v((2, 256, 768)),
        v((256, 512)), v((256, 256)), v((256, 768)), v((256, 768)),
        v((128, 256), F32), v((128, 256), F32),
        v((3, 256, 128)), v((3, 128, 128)),
        v((256, 256)), v((128, 256)), v((256, 256)), v((128, 256)),
        v((128, 512), F32), v((256, 512)), v((256, 512)), v((128, 512)), v((128, 512)),
        v((32, 512)), v((128, 512)),
    ]
    for _ in range(2):
        scratch += [
            v((4, 256, 256)), v((3, 256, 256)), v((8, 32, 256)), v((7, 32, 256)),
            v((2, 16, 256)), v((yc, 16, 256)),
        ]
    scratch += [v((2, 16, 512))]
    scratch += [
        v((4, 128, 384)), v((3, 128, 384)), v((8, 16, 384)), v((7, 16, 384)),
        v((16, 384)), v((ny - 1, 16, 384)), v((8, 16, 384)), v((4, 128, 384)), v((4, 128, 384)),
    ]
    remote = 96
    scratch += [
        pltpu.SemaphoreType.DMA((remote,)),
        pltpu.SemaphoreType.DMA((remote,)),
        pltpu.SemaphoreType.DMA((24,)),
    ]
    anyspace = pl.BlockSpec(memory_space=pl.ANY)
    return pl.pallas_call(
        functools.partial(kernel, ny, factor),
        out_shape=(
            jax.ShapeDtypeStruct((1, 128, 512), BF),
            jax.ShapeDtypeStruct((2, 16, 512), BF),
            jax.ShapeDtypeStruct((2, 256, 768), BF),
        ),
        in_specs=[anyspace] * 5,
        out_specs=(anyspace,) * 3,
        scratch_shapes=scratch,
        compiler_params=pltpu.CompilerParams(collective_id=0, has_side_effects=True),
        name="step",
    )(signal, conv_weight, res_weight, grad_out, skip_cotangent)


def solution(mesh):
    split = Mesh(mesh.devices.reshape(mesh.shape["dp"], NX, NZ, NC), ("dp", *TM))
    return jax.shard_map(
        body,
        mesh=split,
        in_specs=(P("dp", TM, None), P(), P(), P("dp", TM, None), P("dp", TM, None)),
        out_specs=(P("dp", TM, None), P(None, TM, None), P()),
        check_vma=False,
    )
```

```python
import functools

import jax
import jax.numpy as jnp
from jax import lax
from jax.experimental import pallas as pl
from jax.experimental.pallas import tpu as pltpu
from jax.sharding import Mesh
from jax.sharding import PartitionSpec as P

TM = ("tm_0", "tm_1", "tm_2")
NX, NZ, NC = 4, 8, 2
MESH = pl.DeviceIdType.MESH
BF = jnp.bfloat16
F32 = jnp.float32


def mm(a, b):
    return jnp.dot(a, b, preferred_element_type=F32)


def mm_t(a, b):
    return lax.dot_general(a, b, (((1,), (1,)), ((), ())), preferred_element_type=F32)


def t_mm(a, b):
    return lax.dot_general(a, b, (((0,), (0,)), ((), ())), preferred_element_type=F32)


def do_if(cond, action):
    if cond is None:
        action()
    else:
        pl.when(cond)(action)


class Group:
    def __init__(self, link, ref, send_if=None, recv_if=None):
        self.send, self.recv = link.send.at[link.n_remote], link.recv.at[link.n_remote]
        link.n_remote += 1
        link.groups.append(self)
        self.ref, self.device = ref, link.device
        self.send_if, self.recv_if = send_if, recv_if

    def copy(self, src, dst, device):
        return pltpu.make_async_remote_copy(
            src_ref=src,
            dst_ref=dst,
            send_sem=self.send,
            recv_sem=self.recv,
            device_id=device,
            device_id_type=MESH,
        )

    def push(self, src, dst, device):
        do_if(self.send_if, lambda: self.copy(src, dst, device).start())
        return self

    def wait(self):
        do_if(self.recv_if, lambda: self.copy(self.ref, self.ref, self.device).wait_recv())

    def wait_sent(self):
        do_if(self.send_if, lambda: self.copy(self.ref, self.ref, self.device).wait_send())


class Links:
    def __init__(self, send, recv, local, device):
        self.send, self.recv, self.local, self.device = send, recv, local, device
        self.n_remote = self.n_local = 0
        self.groups = []
        self.stored = []

    def push(self, src, dst, device, send_if=None, recv_if=None, ref=None):
        return Group(self, dst if ref is None else ref, send_if, recv_if).push(src, dst, device)

    def move(self, src, dst, last=False):
        i = self.n_local
        self.n_local += 1
        copy = pltpu.make_async_copy(src, dst, self.local.at[i])
        copy.start()
        if last:
            self.stored.append(copy)
        return copy

    def finish(self):
        for group in self.groups:
            group.wait_sent()
        for copy in self.stored:
            copy.wait()


def kernel(
    ny, factor,
    sig, cw, rw, go_in, sk_in,
    ig_out, cg_out, rg_out,
    x0, p0, w, r, go, sk, x1, p1, h0, tf0, sg0, hk, hs, dz1, dz1s, dz0, dz0s,
    gp, o0, dp, dpr, dp0, dp0r, igv,
    cs1, cy1, cx1, cxr1, cz1, czr1, cg1,
    cs0, cx0, cz0, czr0, cy0, cyr0, cgv,
    sa, sb, rgo,
    send, recv, local,
):
    y = lax.axis_index("dp")
    x = lax.axis_index("tm_0")
    z = lax.axis_index("tm_1")
    c = lax.axis_index("tm_2")
    t = x * (NZ * NC) + z * NC + c
    nt = NX * NZ * NC
    near = 32
    far = 8
    rows, width = 128, 512
    gated = 256
    half = gated // 2

    def at(dy=0, dx=0, dz=0, dc=0):
        return (
            lax.rem(y + dy, ny), lax.rem(x + dx, NX), lax.rem(z + dz, NZ), lax.rem(c + dc, NC)
        )

    def along(d):
        s = lax.rem(t + (d + nt), nt)
        return (y, s // (NZ * NC), lax.rem(s // NC, NZ), lax.rem(s, NC))

    partner = at(dc=1)
    xs = [at(dx=d) for d in range(1, NX)]
    zs = [at(dz=d) for d in range(1, NZ)]
    ys = [at(dy=d) for d in range(1, ny)]
    yo = [at(dy=d, dc=1) for d in range(ny)]

    link = Links(send, recv, local, partner)
    own, other = pl.ds(0, rows), pl.ds(rows, rows)
    high = pl.ds(near, rows - near)
    low = pl.ds(0, near)
    in_x = link.move(sig.at[0], x0.at[own])
    in_p = link.move(sig.at[0, pl.ds(0, rows - near)], p0.at[high])
    in_w0 = link.move(cw.at[0], w.at[0])
    in_r0 = link.move(rw.at[0], r.at[0])

    barrier = pltpu.get_barrier_semaphore()
    has = {d: (t + d >= 0) & (t + d < nt) for d in (far, -far, 1, -1)}
    greeted = zs + ys + yo + xs

    def greet(device):
        pl.semaphore_signal(barrier, inc=1, device_id=device, device_id_type=MESH)

    for d in (far, -far):
        do_if(has[d], functools.partial(greet, along(d)))
    for device in greeted:
        greet(device)
    count = len(greeted)
    for d in (1, -1):
        do_if(has[d], functools.partial(greet, along(d)))
    for d in (far, -far, 1, -1):
        count = count + has[d].astype(jnp.int32)

    in_go = link.move(go_in.at[0], go.at[own])
    in_sk = link.move(sk_in.at[0], sk.at[own])
    in_r1 = link.move(rw.at[1], r.at[1])
    in_w1 = link.move(cw.at[1], w.at[1])

    def layer0(lo, n):
        part = pl.ds(lo, n)
        zv = mm(p0[part, :], w[0, 0:width, :]) + mm(x0[part, :], w[0, width : 2 * width, :])
        tf = jnp.tanh(zv[:, :gated])
        sg = jax.nn.sigmoid(zv[:, gated:])
        h = (tf * sg).astype(BF)
        tf0[part, :] = tf
        sg0[part, :] = sg
        h0[part, :] = h
        x1[part, :] = (x0[part, :].astype(F32) + mm(h, r[0, :, 0:width])).astype(BF)

    def cleared(ref):
        def clear():
            ref[...] = jnp.zeros(ref.shape, ref.dtype)

        return clear

    do_if(t == 0, cleared(p0.at[low]))
    do_if(t == nt - 1, cleared(dp0r))
    do_if(t >= nt - far, cleared(dpr))
    do_if(t < far, cleared(p1.at[own]))

    in_x.wait()
    in_p.wait()
    in_w0.wait()
    in_r0.wait()
    layer0(near, rows - near)
    in_go.wait()
    in_sk.wait()

    pl.semaphore_wait(barrier, count)
    halo = link.push(x0.at[pl.ds(rows - near, near)], p0.at[low], along(1), has[1], has[-1])
    far_high = link.push(x1.at[high], p1.at[high], along(far), has[far], has[-far])

    in_r1.wait()
    in_w1.wait()
    e1 = mm_t(go[own, :], r[1, :, 0:width]) + mm_t(sk[own, :], r[1, :, width:])
    es0 = mm_t(sk[own, :], r[0, :, width:])

    halo.wait()
    layer0(0, near)
    far_low = link.push(x1.at[low], p1.at[low], along(far), has[far], has[-far])
    first = c == 0
    hk[0, own, :] = jnp.where(first, h0[:, :half], h0[:, half:])
    hs[0] = jnp.where(first, h0[:, half:], h0[:, :half])
    zc1 = mm(x1[own, :], w[1, width : 2 * width, :])

    far_high.wait()
    far_low.wait()
    go_there = link.push(go.at[own], go.at[other], partner)
    sk_there = link.push(sk.at[own], sk.at[other], partner)
    h0_there = link.push(hs.at[0], hk.at[0, other, :], partner)
    x1_there = link.push(x1.at[own], x1.at[other], partner)
    p1_there = link.push(p1.at[own], p1.at[other], partner)
    x0_there = link.push(x0.at[own], x0.at[other], partner)
    p0_there = link.push(p0.at[own], p0.at[other], partner)
    z1 = zc1 + mm(p1[own, :], w[1, 0:width, :])
    tf = jnp.tanh(z1[:, :gated])
    sg = jax.nn.sigmoid(z1[:, gated:])
    h1 = (tf * sg).astype(BF)
    dza = (e1 * sg * (1.0 - tf * tf)).astype(BF)
    dzb = (e1 * tf * sg * (1.0 - sg)).astype(BF)
    dpast = mm_t(dza, w[1, 0:width, 0:gated]) + mm_t(dzb, w[1, 0:width, gated:])
    dp[...] = dpast.astype(BF)
    back = link.push(dp, dpr, along(-far), has[-far], has[far])
    hk[1, own, :] = jnp.where(first, h1[:, :half], h1[:, half:])
    hs[1] = jnp.where(first, h1[:, half:], h1[:, :half])
    h1_there = link.push(hs.at[1], hk.at[1, other, :], partner)
    dz1[own, :] = jnp.where(first, dza, dzb)
    dz1s[...] = jnp.where(first, dzb, dza)
    dz1_there = link.push(dz1s, dz1.at[other], partner)
    wc = mm_t(dza, w[1, width : 2 * width, 0:gated])
    g = go[own, :].astype(F32) + (wc + mm_t(dzb, w[1, width : 2 * width, gated:]))
    gp[...] = g

    def to_x(src, dst):
        group = Group(link, dst)
        for d in range(1, NX):
            group.push(src.at[lax.rem(x + d, NX)], dst.at[d - 1], xs[d - 1])
        return group

    def to_z(src, dst):
        group = Group(link, dst)
        for d in range(1, NZ):
            group.push(src.at[lax.rem(z + d, NZ)], dst.at[d - 1], zs[d - 1])
        return group

    def to_all(src, dst, devices):
        group = Group(link, dst)
        for i, device in enumerate(devices):
            group.push(src, dst.at[i], device)
        return group

    def to_same(ref, i, devices):
        group = Group(link, ref.at[pl.ds(0, len(devices))])
        for device in devices:
            group.push(ref.at[i], ref.at[i], device)
        return group

    def summed(group, own_part, slots):
        group.wait()
        total = own_part.astype(F32)
        for i in range(slots.shape[0]):
            total = total + slots[i].astype(F32)
        return total

    def res_parts(v, buffers):
        parts, slots = buffers[:2]
        cols = v.shape[1] // 2
        for i in range(NX):
            top, left = 64 * (i // 2), cols * (i % 2)
            piece = v[top : top + 64, left : left + cols]
            parts[i] = piece.reshape(8, 8, cols).astype(BF)
        return to_x(parts, slots)

    def res_to_z(copies, buffers):
        parts, slots, out, out_slots = buffers[:4]
        out[...] = summed(copies, parts[x], slots).astype(BF)
        return to_z(out, out_slots)

    def res_to_y(copies, buffers):
        parts, slots, out, out_slots = buffers[2:6]
        out[...] = summed(copies, parts[z], slots).astype(BF)
        return to_all(out, out_slots, ys)

    def res_to_all_z(copies, buffers):
        part, slots, out = buffers[4:7]
        out[z] = (summed(copies, part[...], slots) * factor).astype(BF)
        return to_same(out, z, zs)

    def res_to_all_x(group, buffers):
        part, out, there = buffers[6:9]
        group.wait()
        out[x] = part[...]
        sends = to_same(out, x, xs)
        return sends, link.push(out.at[x], there.at[x], partner, ref=there)

    def res_to_core(state, buffers):
        out, there = buffers[7:9]
        group, sends = state
        group.wait()
        for d in range(1, NX):
            other_x = lax.rem(x + d, NX)
            sends.push(out.at[other_x], there.at[other_x], partner)
        return sends

    def res_pieces(copies, buffers):
        copies.wait()
        for src, core in ((buffers[7], c), (buffers[8], 1 - c)):
            for i in range(NX):
                v = src[i].astype(F32)
                v = v.reshape(64, v.shape[-1]).astype(BF)
                yield pl.ds(pl.multiple_of(core * half + 64 * (i // 2), 64), 64), i % 2, v

    go_there.wait()
    sk_there.wait()
    h0_there.wait()
    h1_there.wait()
    both = [t_mm(hk[1], go[...]), t_mm(hk[1], sk[...]), t_mm(hk[0], sk[...])]
    resa_x = res_parts(jnp.concatenate(both, axis=1), sa)

    def conv_parts(past, cur, dz, out):
        dzv = dz[...]
        for i in range(NX):
            src = past if i < 2 else cur
            col = (i % 2) * 256
            v = t_mm(src[:, col : col + 256], dzv).astype(BF)
            for k in range(NZ):
                for core in range(NC):
                    at_row = 32 * k + 16 * core
                    out[lax.rem(core + c + 1, NC), i, k] = v[at_row : at_row + 16, :]

    def conv_to_x(src, dst):
        return [to_x(src.at[j], dst.at[j]) for j in range(NC)]

    def conv_to_z(j, copies, parts, slots, out, out_slots):
        out[j] = summed(copies[j], parts[j, x], slots.at[j]).astype(BF)
        return to_z(out.at[j], out_slots.at[j])

    def conv_to_y(j, copies, parts, slots, out, out_slots):
        out[j] = summed(copies, parts[j, z], slots.at[j]).astype(BF)
        devices = ys if j else yo
        return to_all(out.at[j], out_slots.at[j, pl.ds(0, len(devices))], devices)

    def conv_final(layer, copies, part, slots):
        mine = summed(copies[1], part[1], slots.at[1, pl.ds(0, ny - 1)])
        theirs = summed(copies[0], jnp.zeros((16, 256), F32), slots.at[0])
        cgv[layer, :, 0:256] = (jnp.where(first, mine, theirs) * factor).astype(BF)
        cgv[layer, :, 256:512] = (jnp.where(first, theirs, mine) * factor).astype(BF)

    dz1_there.wait()
    x1_there.wait()
    p1_there.wait()
    dzv = dz1[...]
    for i in range(NX):
        src = p1 if i < 2 else x1
        col = (i % 2) * 256
        v = t_mm(src[:, col : col + 256], dzv).reshape(NZ, 4, 8, 256)
        for k in range(8):
            cs1[k, i] = v[:, k // 2, :, 128 * (k % 2) : 128 * (k % 2) + 128].astype(BF)
    conv1_y = Group(link, cy1)
    for d in range(1, ny):
        conv1_y.push(cs1.at[lax.rem(y + d, ny)], cy1.at[d - 1], ys[d - 1])
    back.wait()
    g1 = gp[...] + dpr[...].astype(F32)
    o0[own, :] = g1.astype(BF)
    o0_there = link.push(o0.at[own], o0.at[other], partner)
    e0 = mm_t(o0[own, :], r[0, :, 0:width]) + es0
    tf = tf0[...]
    sg = sg0[...]
    dza = (e0 * sg * (1.0 - tf * tf)).astype(BF)
    dzb = (e0 * tf * sg * (1.0 - sg)).astype(BF)
    dz0[own, :] = jnp.where(first, dza, dzb)
    dz0s[...] = jnp.where(first, dzb, dza)
    dz0_there = link.push(dz0s, dz0.at[other], partner)
    dpast = (mm_t(dza, w[0, 0:width, 0:gated]) + mm_t(dzb, w[0, 0:width, gated:])).astype(BF)
    dp0[...] = dpast
    halo_back = link.push(dp0.at[low], dp0r, along(-1), has[-1], has[1])
    resa_z = res_to_z(resa_x, sa)
    o0_there.wait()
    resb_x = res_parts(t_mm(hk[0], o0[...]), sb)
    x0_there.wait()
    p0_there.wait()
    dz0_there.wait()
    conv_parts(p0, x0, dz0, cs0)
    conv0_x = conv_to_x(cs0, cx0)
    wc = mm_t(dza, w[0, width : 2 * width, 0:gated]) + mm_t(dzb, w[0, width : 2 * width, gated:])
    halo_back.wait()
    moved = jnp.concatenate([dp0[near:, :], dp0r[...]], axis=0).astype(F32)
    igv[...] = (g1 + wc + moved).astype(BF)
    link.move(igv, ig_out.at[0], last=True)
    resb_z = res_to_z(resb_x, sb)
    resa_y = res_to_y(resa_z, sa)
    cx1[...] = summed(conv1_y, cs1[y], cy1).astype(BF)
    conv1_x = to_x(cx1, cxr1)
    conv0_z = [conv_to_z(j, conv0_x, cs0, cx0, cz0, czr0) for j in range(NC)]
    cz1[...] = summed(conv1_x, cx1[x], cxr1).astype(BF)
    conv1_z = to_z(cz1, czr1)
    resb_y = res_to_y(resb_z, sb)
    resa_gz = res_to_all_z(resa_y, sa)
    conv0_y = [conv_to_y(j, conv0_z[j], cz0, czr0, cy0, cyr0) for j in range(NC)]
    resb_gz = res_to_all_z(resb_y, sb)
    cg1[c * ny + y] = (summed(conv1_z, cz1[z], czr1) * factor).astype(BF)
    piece = c * ny + y
    conv1_g = to_same(cg1, piece, ys + yo)
    resa_gx = res_to_all_x(resa_gz, sa)
    resb_gx = res_to_all_x(resb_gz, sb)
    conv_final(0, conv0_y, cy0, cyr0)
    conv1_g.wait()
    for core in range(NC):
        for k in range(4):
            left = 256 * core + 128 * (k % 2)
            top = 8 * (k // 2)
            cgv[1, top : top + 8, left : left + 128] = cg1[ny * core + 4 * c + k]
    link.move(cgv, cg_out, last=True)
    resa_gc = res_to_core(resa_gx, sa)
    for place, side, v in res_pieces(resa_gc, sa):
        if side:
            rgo[1, place, width:] = v[:, :256]
            rgo[0, place, width:] = v[:, 256:]
        else:
            rgo[1, place, 0:width] = v
    link.move(rgo.at[1], rg_out.at[1], last=True)
    resb_gc = res_to_core(resb_gx, sb)
    for place, side, v in res_pieces(resb_gc, sb):
        rgo[0, place, 256 * side : 256 * side + 256] = v
    link.move(rgo.at[0], rg_out.at[0], last=True)
    link.finish()


def store(a, b, c, a_out, b_out, c_out, sems):
    copies = [
        pltpu.make_async_copy(src, dst, sems.at[i])
        for i, (src, dst) in enumerate(((a, a_out), (b, b_out), (c, c_out)))
    ]
    for copy in copies:
        copy.start()
    for copy in copies:
        copy.wait()


def body(signal, conv_weight, res_weight, grad_out, skip_cotangent):
    ny = lax.axis_size("dp")
    total = signal.shape[0] * signal.shape[1] * ny * lax.axis_size(TM)
    factor = float(total) ** (-0.5)

    def v(shape, dtype=BF):
        return pltpu.VMEM(shape, dtype)

    def res_scratch(cols):
        return [
            v((4, 8, 8, cols)), v((3, 8, 8, cols)), v((8, 8, cols)), v((7, 8, cols)),
            v((8, cols)), v((ny - 1, 8, cols)), v((8, 8, cols)), v((4, 8, 8, cols)),
            v((4, 8, 8, cols)),
        ]

    remote = 42
    scratch = [
        v((256, 512)), v((256, 512)), v((2, 1024, 512)), v((2, 256, 768)),
        v((256, 512)), v((256, 256)), v((256, 512)), v((256, 512)), v((128, 256)),
        v((128, 256), F32), v((128, 256), F32),
        v((2, 256, 128)), v((2, 128, 128)),
        v((256, 256)), v((128, 256)), v((256, 256)), v((128, 256)),
        v((128, 512), F32), v((256, 512)), v((128, 512)), v((128, 512)), v((128, 512)),
        v((32, 512)), v((128, 512)),
        v((ny, 4, 8, 8, 128)), v((ny - 1, 4, 8, 8, 128)), v((4, 8, 8, 128)), v((3, 8, 8, 128)),
        v((8, 8, 128)), v((7, 8, 128)), v((2 * ny, 8, 128)),
        v((2, 4, 8, 16, 256)), v((2, 3, 8, 16, 256)), v((2, 8, 16, 256)), v((2, 7, 16, 256)),
        v((2, 16, 256)), v((2, ny, 16, 256)), v((2, 16, 512)),
        res_scratch(512), res_scratch(256), v((2, 256, 768)),
        pltpu.SemaphoreType.DMA((remote,)),
        pltpu.SemaphoreType.DMA((remote,)),
        pltpu.SemaphoreType.DMA((12,)),
    ]
    anyspace = pl.BlockSpec(memory_space=pl.ANY)
    results = pl.pallas_call(
        functools.partial(kernel, ny, factor),
        out_shape=(
            jax.ShapeDtypeStruct((1, 128, 512), BF),
            jax.ShapeDtypeStruct((2, 16, 512), BF),
            jax.ShapeDtypeStruct((2, 256, 768), BF),
        ),
        in_specs=[anyspace] * 5,
        out_specs=(anyspace,) * 3,
        scratch_shapes=scratch,
        compiler_params=pltpu.CompilerParams(collective_id=0, has_side_effects=True),
        name="step",
    )(signal, conv_weight, res_weight, grad_out, skip_cotangent)
    return pl.pallas_call(
        store,
        out_shape=tuple(jax.ShapeDtypeStruct(a.shape, a.dtype) for a in results),
        in_specs=[pl.BlockSpec(memory_space=pltpu.VMEM)] * 3,
        out_specs=(anyspace,) * 3,
        scratch_shapes=[pltpu.SemaphoreType.DMA((3,))],
        name="store",
    )(*results)


def solution(mesh):
    split = Mesh(mesh.devices.reshape(mesh.shape["dp"], NX, NZ, NC), ("dp", *TM))
    return jax.shard_map(
        body,
        mesh=split,
        in_specs=(P("dp", TM, None), P(), P(), P("dp", TM, None), P("dp", TM, None)),
        out_specs=(P("dp", TM, None), P(None, TM, None), P()),
        check_vma=False,
    )
```

```python
import functools

import jax
import jax.numpy as jnp
from jax import lax
from jax.experimental import pallas as pl
from jax.experimental.pallas import tpu as pltpu
from jax.sharding import Mesh
from jax.sharding import PartitionSpec as P

TM = ("tm_0", "tm_1", "tm_2")
NX, NZ, NC = 4, 8, 2
MESH = pl.DeviceIdType.MESH
BF = jnp.bfloat16
F32 = jnp.float32


def mm(a, b):
    return jnp.dot(a, b, preferred_element_type=F32)


def mm_t(a, b):
    return lax.dot_general(a, b, (((1,), (1,)), ((), ())), preferred_element_type=F32)


def t_mm(a, b):
    return lax.dot_general(a, b, (((0,), (0,)), ((), ())), preferred_element_type=F32)


def do_if(cond, action):
    if cond is None:
        action()
    else:
        pl.when(cond)(action)


class Group:
    def __init__(self, link, ref, send_if=None, recv_if=None):
        self.send, self.recv = link.send.at[link.n_remote], link.recv.at[link.n_remote]
        link.n_remote += 1
        link.groups.append(self)
        self.ref, self.device = ref, link.device
        self.send_if, self.recv_if = send_if, recv_if

    def copy(self, src, dst, device):
        return pltpu.make_async_remote_copy(
            src_ref=src,
            dst_ref=dst,
            send_sem=self.send,
            recv_sem=self.recv,
            device_id=device,
            device_id_type=MESH,
        )

    def push(self, src, dst, device):
        do_if(self.send_if, lambda: self.copy(src, dst, device).start())
        return self

    def wait(self):
        do_if(self.recv_if, lambda: self.copy(self.ref, self.ref, self.device).wait_recv())

    def wait_sent(self):
        do_if(self.send_if, lambda: self.copy(self.ref, self.ref, self.device).wait_send())


class Links:
    def __init__(self, send, recv, local, device):
        self.send, self.recv, self.local, self.device = send, recv, local, device
        self.n_remote = self.n_local = 0
        self.groups = []
        self.stored = []

    def push(self, src, dst, device, send_if=None, recv_if=None, ref=None):
        return Group(self, dst if ref is None else ref, send_if, recv_if).push(src, dst, device)

    def move(self, src, dst, last=False):
        i = self.n_local
        self.n_local += 1
        copy = pltpu.make_async_copy(src, dst, self.local.at[i])
        copy.start()
        if last:
            self.stored.append(copy)
        return copy

    def finish(self):
        for group in self.groups:
            group.wait_sent()
        for copy in self.stored:
            copy.wait()


def kernel(
    ny, factor,
    sig, cw, rw, go_in, sk_in,
    ig_out, cg_out, rg_out,
    x0, p0, w, r, go, sk, x1, p1, h0, tf0, sg0, hk, hs, dz1, dz1s, dz0, dz0s,
    gp, o0, dp, dpr, dp0, dp0r, igv,
    cs1, cy1, cx1, cxr1, cz1, czr1, cg1,
    mine0, left0, right0, cy0, cyr0, cgv,
    sa, sb, rgo,
    send, recv, local,
):
    y = lax.axis_index("dp")
    x = lax.axis_index("tm_0")
    z = lax.axis_index("tm_1")
    c = lax.axis_index("tm_2")
    t = x * (NZ * NC) + z * NC + c
    nt = NX * NZ * NC
    near = 32
    far = 8
    rows, width = 128, 512
    gated = 256
    half = gated // 2

    def at(dy=0, dx=0, dz=0, dc=0):
        return (
            lax.rem(y + dy, ny), lax.rem(x + dx, NX), lax.rem(z + dz, NZ), lax.rem(c + dc, NC)
        )

    def along(d):
        s = lax.rem(t + (d + nt), nt)
        return (y, s // (NZ * NC), lax.rem(s // NC, NZ), lax.rem(s, NC))

    partner = at(dc=1)
    xs = [at(dx=d) for d in range(1, NX)]
    zs = [at(dz=d) for d in range(1, NZ)]
    ys = [at(dy=d) for d in range(1, ny)]
    yo = [at(dy=d, dc=1) for d in range(ny)]

    link = Links(send, recv, local, partner)
    own, other = pl.ds(0, rows), pl.ds(rows, rows)
    high = pl.ds(near, rows - near)
    low = pl.ds(0, near)
    in_x = link.move(sig.at[0], x0.at[own])
    in_p = link.move(sig.at[0, pl.ds(0, rows - near)], p0.at[high])
    in_w0 = link.move(cw.at[0], w.at[0])
    in_r0 = link.move(rw.at[0], r.at[0])

    barrier = pltpu.get_barrier_semaphore()
    has = {d: (t + d >= 0) & (t + d < nt) for d in (far, -far, 1, -1)}
    greeted = zs + ys + yo + xs

    def greet(device):
        pl.semaphore_signal(barrier, inc=1, device_id=device, device_id_type=MESH)

    for d in (far, -far):
        do_if(has[d], functools.partial(greet, along(d)))
    for device in greeted:
        greet(device)
    count = len(greeted)
    for d in (1, -1):
        do_if(has[d], functools.partial(greet, along(d)))
    for d in (far, -far, 1, -1):
        count = count + has[d].astype(jnp.int32)

    in_go = link.move(go_in.at[0], go.at[own])
    in_sk = link.move(sk_in.at[0], sk.at[own])
    in_r1 = link.move(rw.at[1], r.at[1])
    in_w1 = link.move(cw.at[1], w.at[1])

    def layer0(lo, n):
        part = pl.ds(lo, n)
        zv = mm(p0[part, :], w[0, 0:width, :]) + mm(x0[part, :], w[0, width : 2 * width, :])
        tf = jnp.tanh(zv[:, :gated])
        sg = jax.nn.sigmoid(zv[:, gated:])
        h = (tf * sg).astype(BF)
        tf0[part, :] = tf
        sg0[part, :] = sg
        h0[part, :] = h
        x1[part, :] = (x0[part, :].astype(F32) + mm(h, r[0, :, 0:width])).astype(BF)

    def cleared(ref):
        def clear():
            ref[...] = jnp.zeros(ref.shape, ref.dtype)

        return clear

    do_if(t == 0, cleared(p0.at[low]))
    do_if(t == nt - 1, cleared(dp0r))
    do_if(t >= nt - far, cleared(dpr))
    do_if(t < far, cleared(p1.at[own]))

    in_x.wait()
    in_p.wait()
    in_w0.wait()
    in_r0.wait()
    layer0(near, rows - near)
    in_go.wait()
    in_sk.wait()

    pl.semaphore_wait(barrier, count)
    halo = link.push(x0.at[pl.ds(rows - near, near)], p0.at[low], along(1), has[1], has[-1])
    far_high = link.push(x1.at[high], p1.at[high], along(far), has[far], has[-far])

    in_r1.wait()
    in_w1.wait()
    e1 = mm_t(go[own, :], r[1, :, 0:width]) + mm_t(sk[own, :], r[1, :, width:])
    es0 = mm_t(sk[own, :], r[0, :, width:])

    halo.wait()
    layer0(0, near)
    far_low = link.push(x1.at[low], p1.at[low], along(far), has[far], has[-far])
    first = c == 0
    hk[0, own, :] = jnp.where(first, h0[:, :half], h0[:, half:])
    hs[0] = jnp.where(first, h0[:, half:], h0[:, :half])
    zc1 = mm(x1[own, :], w[1, width : 2 * width, :])

    far_high.wait()
    far_low.wait()
    go_there = link.push(go.at[own], go.at[other], partner)
    sk_there = link.push(sk.at[own], sk.at[other], partner)
    h0_there = link.push(hs.at[0], hk.at[0, other, :], partner)
    x1_there = link.push(x1.at[own], x1.at[other], partner)
    p1_there = link.push(p1.at[own], p1.at[other], partner)
    x0_there = link.push(x0.at[own], x0.at[other], partner)
    p0_there = link.push(p0.at[own], p0.at[other], partner)
    z1 = zc1 + mm(p1[own, :], w[1, 0:width, :])
    tf = jnp.tanh(z1[:, :gated])
    sg = jax.nn.sigmoid(z1[:, gated:])
    h1 = (tf * sg).astype(BF)
    dza = (e1 * sg * (1.0 - tf * tf)).astype(BF)
    dzb = (e1 * tf * sg * (1.0 - sg)).astype(BF)
    dpast = mm_t(dza, w[1, 0:width, 0:gated]) + mm_t(dzb, w[1, 0:width, gated:])
    dp[...] = dpast.astype(BF)
    back = link.push(dp, dpr, along(-far), has[-far], has[far])
    hk[1, own, :] = jnp.where(first, h1[:, :half], h1[:, half:])
    hs[1] = jnp.where(first, h1[:, half:], h1[:, :half])
    h1_there = link.push(hs.at[1], hk.at[1, other, :], partner)
    dz1[own, :] = jnp.where(first, dza, dzb)
    dz1s[...] = jnp.where(first, dzb, dza)
    dz1_there = link.push(dz1s, dz1.at[other], partner)
    wc = mm_t(dza, w[1, width : 2 * width, 0:gated])
    g = go[own, :].astype(F32) + (wc + mm_t(dzb, w[1, width : 2 * width, gated:]))
    gp[...] = g

    def to_x(src, dst):
        group = Group(link, dst)
        for d in range(1, NX):
            group.push(src.at[lax.rem(x + d, NX)], dst.at[d - 1], xs[d - 1])
        return group

    def to_z(src, dst):
        group = Group(link, dst)
        for d in range(1, NZ):
            group.push(src.at[lax.rem(z + d, NZ)], dst.at[d - 1], zs[d - 1])
        return group

    def to_all(src, dst, devices):
        group = Group(link, dst)
        for i, device in enumerate(devices):
            group.push(src, dst.at[i], device)
        return group

    def to_same(ref, i, devices):
        group = Group(link, ref.at[pl.ds(0, len(devices))])
        for device in devices:
            group.push(ref.at[i], ref.at[i], device)
        return group

    def summed(group, own_part, slots):
        group.wait()
        total = own_part.astype(F32)
        for i in range(slots.shape[0]):
            total = total + slots[i].astype(F32)
        return total

    def res_parts(v, buffers):
        parts, slots = buffers[:2]
        cols = v.shape[1] // 2
        for i in range(NX):
            top, left = 64 * (i // 2), cols * (i % 2)
            piece = v[top : top + 64, left : left + cols]
            parts[i] = piece.reshape(8, 8, cols).astype(BF)
        return to_x(parts, slots)

    def res_to_z(copies, buffers):
        parts, slots, out, out_slots = buffers[:4]
        out[...] = summed(copies, parts[x], slots).astype(BF)
        return to_z(out, out_slots)

    def res_direct(v, parts, slots):
        for i in range(NX):
            top, left = 64 * (i // 2), 256 * (i % 2)
            parts[i] = v[top : top + 64, left : left + 256].reshape(8, 8, 256).astype(BF)
        group = Group(link, slots)
        for i in range(1, NX * NZ):
            dx, dz = i // NZ, i % NZ
            src = parts.at[lax.rem(x + dx, NX), lax.rem(z + dz, NZ)]
            group.push(src, slots.at[i - 1], at(dx=dx, dz=dz))
        return group

    def res_to_y(copies, buffers):
        parts, slots, out, out_slots = buffers[2:6]
        out[...] = summed(copies, parts[z], slots).astype(BF)
        return to_all(out, out_slots, ys)

    def res_to_all_z(copies, buffers):
        part, slots, out = buffers[4:7]
        out[z] = (summed(copies, part[...], slots) * factor).astype(BF)
        return to_same(out, z, zs)

    def res_to_all_x(group, buffers):
        part, out, there = buffers[6:9]
        group.wait()
        out[x] = part[...]
        sends = to_same(out, x, xs)
        return sends, link.push(out.at[x], there.at[x], partner, ref=there)

    def res_to_core(state, buffers):
        out, there = buffers[7:9]
        group, sends = state
        group.wait()
        for d in range(1, NX):
            other_x = lax.rem(x + d, NX)
            sends.push(out.at[other_x], there.at[other_x], partner)
        return sends

    def res_pieces(copies, buffers):
        copies.wait()
        for src, core in ((buffers[7], c), (buffers[8], 1 - c)):
            for i in range(NX):
                v = src[i].astype(F32)
                v = v.reshape(64, v.shape[-1]).astype(BF)
                yield pl.ds(pl.multiple_of(core * half + 64 * (i // 2), 64), 64), i % 2, v

    go_there.wait()
    sk_there.wait()
    h0_there.wait()
    h1_there.wait()
    both = [t_mm(hk[1], go[...]), t_mm(hk[1], sk[...]), t_mm(hk[0], sk[...])]
    resa_x = res_parts(jnp.concatenate(both, axis=1), sa)

    def conv_parts(past, cur, dz):
        dzv = dz[...]
        for i in range(NX):
            src = past if i < 2 else cur
            col = (i % 2) * 256
            v = t_mm(src[:, col : col + 256], dzv).reshape(NZ, 2, 16, 256)
            mine0[0][i] = jnp.where(first, v[:, 0], v[:, 1]).astype(BF)
            rest = jnp.where(first, v[:, 1], v[:, 0]).astype(BF)
            left0[0][i] = rest[:, :, :128]
            right0[0][:, i] = rest[:, :, 128:]

    def x_to_z(group, buffers):
        parts, slots, out, out_slots = buffers
        out[...] = summed(group, parts[x], slots).astype(BF)
        return to_z(out, out_slots)

    def z_to_x(group, buffers):
        parts, slots, out, out_slots = buffers
        out[...] = summed(group, parts[z], slots).astype(BF)
        return to_x(out, out_slots)

    def conv_final(layer, copies, part, slots):
        mine = summed(copies[1], part[1], slots.at[1, pl.ds(0, ny - 1)])
        theirs = summed(copies[0], jnp.zeros((16, 256), F32), slots.at[0])
        cgv[layer, :, 0:256] = (jnp.where(first, mine, theirs) * factor).astype(BF)
        cgv[layer, :, 256:512] = (jnp.where(first, theirs, mine) * factor).astype(BF)

    dz1_there.wait()
    x1_there.wait()
    p1_there.wait()
    dzv = dz1[...]
    for i in range(NX):
        src = p1 if i < 2 else x1
        col = (i % 2) * 256
        v = t_mm(src[:, col : col + 256], dzv).reshape(NZ, 4, 8, 256)
        for k in range(8):
            cs1[k, i] = v[:, k // 2, :, 128 * (k % 2) : 128 * (k % 2) + 128].astype(BF)
    conv1_y = Group(link, cy1)
    for d in range(1, ny):
        conv1_y.push(cs1.at[lax.rem(y + d, ny)], cy1.at[d - 1], ys[d - 1])
    resa_z = res_to_z(resa_x, sa)
    back.wait()
    g1 = gp[...] + dpr[...].astype(F32)
    o0[own, :] = g1.astype(BF)
    o0_there = link.push(o0.at[own], o0.at[other], partner)
    e0 = mm_t(o0[own, :], r[0, :, 0:width]) + es0
    tf = tf0[...]
    sg = sg0[...]
    dza = (e0 * sg * (1.0 - tf * tf)).astype(BF)
    dzb = (e0 * tf * sg * (1.0 - sg)).astype(BF)
    dz0[own, :] = jnp.where(first, dza, dzb)
    dz0s[...] = jnp.where(first, dzb, dza)
    dz0_there = link.push(dz0s, dz0.at[other], partner)
    dpast = (mm_t(dza, w[0, 0:width, 0:gated]) + mm_t(dzb, w[0, 0:width, gated:])).astype(BF)
    dp0[...] = dpast
    halo_back = link.push(dp0.at[low], dp0r, along(-1), has[-1], has[1])
    o0_there.wait()
    resb_x = res_direct(t_mm(hk[0], o0[...]), sb[0], sb[1])
    x0_there.wait()
    p0_there.wait()
    dz0_there.wait()
    conv_parts(p0, x0, dz0)
    right_z = to_z(right0[0], right0[1])
    mine_x = to_x(mine0[0], mine0[1])
    left_x = to_x(left0[0], left0[1])
    wc = mm_t(dza, w[0, width : 2 * width, 0:gated]) + mm_t(dzb, w[0, width : 2 * width, gated:])
    halo_back.wait()
    moved = jnp.concatenate([dp0[near:, :], dp0r[...]], axis=0).astype(F32)
    igv[...] = (g1 + wc + moved).astype(BF)
    link.move(igv, ig_out.at[0], last=True)
    resa_y = res_to_y(resa_z, sa)
    cx1[...] = summed(conv1_y, cs1[y], cy1).astype(BF)
    conv1_x = to_x(cx1, cxr1)
    mine_z = x_to_z(mine_x, mine0)
    left_z = x_to_z(left_x, left0)
    right_x = z_to_x(right_z, right0)
    sb[4][...] = summed(resb_x, sb[0][x, z], sb[1]).astype(BF)
    resb_y = to_all(sb[4], sb[5], ys)
    cz1[...] = summed(conv1_x, cx1[x], cxr1).astype(BF)
    conv1_z = to_z(cz1, czr1)
    resa_gz = res_to_all_z(resa_y, sa)
    cy0[1] = summed(mine_z, mine0[2][z], mine0[3]).astype(BF)
    mine_y = to_all(cy0.at[1], cyr0.at[1, pl.ds(0, ny - 1)], ys)
    resb_gz = res_to_all_z(resb_y, sb)
    cy0[0, :, 0:128] = summed(left_z, left0[2][z], left0[3]).astype(BF)
    cy0[0, :, 128:256] = summed(right_x, right0[2][x], right0[3]).astype(BF)
    rest_y = to_all(cy0.at[0], cyr0.at[0], yo)
    cg1[c * ny + y] = (summed(conv1_z, cz1[z], czr1) * factor).astype(BF)
    piece = c * ny + y
    conv1_g = to_same(cg1, piece, ys + yo)
    resa_gx = res_to_all_x(resa_gz, sa)
    resb_gx = res_to_all_x(resb_gz, sb)
    conv_final(0, (rest_y, mine_y), cy0, cyr0)
    conv1_g.wait()
    for core in range(NC):
        for k in range(4):
            left = 256 * core + 128 * (k % 2)
            top = 8 * (k // 2)
            cgv[1, top : top + 8, left : left + 128] = cg1[ny * core + 4 * c + k]
    link.move(cgv, cg_out, last=True)
    resa_gc = res_to_core(resa_gx, sa)
    for place, side, v in res_pieces(resa_gc, sa):
        if side:
            rgo[1, place, width:] = v[:, :256]
            rgo[0, place, width:] = v[:, 256:]
        else:
            rgo[1, place, 0:width] = v
    link.move(rgo.at[1], rg_out.at[1], last=True)
    resb_gc = res_to_core(resb_gx, sb)
    for place, side, v in res_pieces(resb_gc, sb):
        rgo[0, place, 256 * side : 256 * side + 256] = v
    link.move(rgo.at[0], rg_out.at[0], last=True)
    link.finish()


def store(*refs):
    n = (len(refs) - 2) // 3
    srcs, dsts, kept = refs[:n], refs[n : 2 * n], refs[2 * n : 3 * n]
    came, went = refs[-2:]
    parts = [(a, i) for a in range(n) for i in range(srcs[a].shape[0])]
    loads = [
        pltpu.make_async_copy(srcs[a].at[i], kept[a].at[i], came.at[k])
        for k, (a, i) in enumerate(parts)
    ]
    stores = [
        pltpu.make_async_copy(kept[a].at[i], dsts[a].at[i], went.at[k])
        for k, (a, i) in enumerate(parts)
    ]
    for load in loads:
        load.start()
    for load, out in zip(loads, stores):
        load.wait()
        out.start()
    for out in stores:
        out.wait()


def body(signal, conv_weight, res_weight, grad_out, skip_cotangent):
    ny = lax.axis_size("dp")
    total = signal.shape[0] * signal.shape[1] * ny * lax.axis_size(TM)
    factor = float(total) ** (-0.5)

    def v(shape, dtype=BF):
        return pltpu.VMEM(shape, dtype)

    def res_scratch(cols, first):
        return [
            v((4, 8, 8, cols)), v((*first, 8, cols)), v((8, 8, cols)), v((7, 8, cols)),
            v((8, cols)), v((ny - 1, 8, cols)), v((8, 8, cols)), v((4, 8, 8, cols)),
            v((4, 8, 8, cols)),
        ]

    remote = 42
    scratch = [
        v((256, 512)), v((256, 512)), v((2, 1024, 512)), v((2, 256, 768)),
        v((256, 512)), v((256, 256)), v((256, 512)), v((256, 512)), v((128, 256)),
        v((128, 256), F32), v((128, 256), F32),
        v((2, 256, 128)), v((2, 128, 128)),
        v((256, 256)), v((128, 256)), v((256, 256)), v((128, 256)),
        v((128, 512), F32), v((256, 512)), v((128, 512)), v((128, 512)), v((128, 512)),
        v((32, 512)), v((128, 512)),
        v((ny, 4, 8, 8, 128)), v((ny - 1, 4, 8, 8, 128)), v((4, 8, 8, 128)), v((3, 8, 8, 128)),
        v((8, 8, 128)), v((7, 8, 128)), v((2 * ny, 8, 128)),
        [v((4, 8, 16, 256)), v((3, 8, 16, 256)), v((8, 16, 256)), v((7, 16, 256))],
        [v((4, 8, 16, 128)), v((3, 8, 16, 128)), v((8, 16, 128)), v((7, 16, 128))],
        [v((8, 4, 16, 128)), v((7, 4, 16, 128)), v((4, 16, 128)), v((3, 16, 128))],
        v((2, 16, 256)), v((2, ny, 16, 256)), v((2, 16, 512)),
        res_scratch(512, (3, 8)), res_scratch(256, (31,)), v((2, 256, 768)),
        pltpu.SemaphoreType.DMA((remote,)),
        pltpu.SemaphoreType.DMA((remote,)),
        pltpu.SemaphoreType.DMA((12,)),
    ]
    anyspace = pl.BlockSpec(memory_space=pl.ANY)
    results = pl.pallas_call(
        functools.partial(kernel, ny, factor),
        out_shape=(
            jax.ShapeDtypeStruct((1, 128, 512), BF),
            jax.ShapeDtypeStruct((2, 16, 512), BF),
            jax.ShapeDtypeStruct((2, 256, 768), BF),
        ),
        in_specs=[anyspace] * 5,
        out_specs=(anyspace,) * 3,
        scratch_shapes=scratch,
        compiler_params=pltpu.CompilerParams(collective_id=0, has_side_effects=True),
        name="step",
    )(signal, conv_weight, res_weight, grad_out, skip_cotangent)
    n = sum(a.shape[0] for a in results)
    return pl.pallas_call(
        store,
        out_shape=tuple(jax.ShapeDtypeStruct(a.shape, a.dtype) for a in results),
        in_specs=[anyspace] * 3,
        out_specs=(anyspace,) * 3,
        scratch_shapes=[v(a.shape) for a in results] + [pltpu.SemaphoreType.DMA((n,))] * 2,
        name="store",
    )(*results)


def solution(mesh):
    split = Mesh(mesh.devices.reshape(mesh.shape["dp"], NX, NZ, NC), ("dp", *TM))
    return jax.shard_map(
        body,
        mesh=split,
        in_specs=(P("dp", TM, None), P(), P(), P("dp", TM, None), P("dp", TM, None)),
        out_specs=(P("dp", TM, None), P(None, TM, None), P()),
        check_vma=False,
    )
```

```python
import functools
import math

import jax
import jax.numpy as jnp
from jax import lax
from jax.experimental import pallas as pl
from jax.experimental.pallas import tpu as pltpu
from jax.sharding import Mesh
from jax.sharding import PartitionSpec as P

TM = ("tm_0", "tm_1", "tm_2")
NX, NZ, NC = 4, 8, 2
MESH = pl.DeviceIdType.MESH
BF = jnp.bfloat16
F32 = jnp.float32


def mm(a, b):
    return jnp.dot(a, b, preferred_element_type=F32)


def mm_t(a, b):
    return lax.dot_general(a, b, (((1,), (1,)), ((), ())), preferred_element_type=F32)


def t_mm(a, b):
    return lax.dot_general(a, b, (((0,), (0,)), ((), ())), preferred_element_type=F32)


def do_if(cond, action):
    if cond is None:
        action()
    else:
        pl.when(cond)(action)


class Group:
    def __init__(self, link, ref, send_if=None, recv_if=None):
        self.recv = link.recv.at[link.n_remote]
        link.n_remote += 1
        if send_if is None:
            self.send = link.send.at[0]
            link.total += math.prod(ref.shape)
        else:
            link.groups.append(self)
            self.send = link.send.at[len(link.groups)]
        self.ref, self.device = ref, link.device
        self.send_if, self.recv_if = send_if, recv_if

    def copy(self, src, dst, device):
        return pltpu.make_async_remote_copy(
            src_ref=src,
            dst_ref=dst,
            send_sem=self.send,
            recv_sem=self.recv,
            device_id=device,
            device_id_type=MESH,
        )

    def push(self, src, dst, device):
        do_if(self.send_if, lambda: self.copy(src, dst, device).start())
        return self

    def wait(self):
        do_if(self.recv_if, lambda: self.copy(self.ref, self.ref, self.device).wait_recv())

    def wait_sent(self):
        do_if(self.send_if, lambda: self.copy(self.ref, self.ref, self.device).wait_send())


class Links:
    def __init__(self, send, recv, local, device, spare):
        self.send, self.recv, self.local, self.device = send, recv, local, device
        self.spare = spare
        self.n_remote = self.n_local = self.total = 0
        self.groups = []
        self.stored = []

    def push(self, src, dst, device, send_if=None, recv_if=None, ref=None):
        return Group(self, dst if ref is None else ref, send_if, recv_if).push(src, dst, device)

    def move(self, src, dst, last=False):
        i = self.n_local
        self.n_local += 1
        copy = pltpu.make_async_copy(src, dst, self.local.at[i])
        copy.start()
        if last:
            self.stored.append(copy)
        return copy

    def finish(self):
        for group in self.groups:
            group.wait_sent()
        assert self.total % 256 == 0
        pltpu.make_async_remote_copy(
            src_ref=self.spare.at[pl.ds(0, self.total // 256)],
            dst_ref=self.spare.at[pl.ds(0, self.total // 256)],
            send_sem=self.send.at[0],
            recv_sem=self.recv.at[0],
            device_id=self.device,
            device_id_type=MESH,
        ).wait_send()
        for copy in self.stored:
            copy.wait()


def kernel(
    ny, factor,
    sig, cw, rw, go_in, sk_in,
    ig_out, cg_out, rg_out,
    x0, p0, w, r, go, sk, x1, p1, h0, tf0, sg0, hk, hs, dz1, dz1s, dz0, dz0s,
    gp, o0, dp, dpr, dp0, dp0r, igv,
    cs1, cy1, cx1, cxr1, cz1, czr1, cg1,
    mine0, left0, right0, cy0, cyr0, cgv,
    sa, sb, rgo, spare,
    send, recv, local,
):
    y = lax.axis_index("dp")
    x = lax.axis_index("tm_0")
    z = lax.axis_index("tm_1")
    c = lax.axis_index("tm_2")
    t = x * (NZ * NC) + z * NC + c
    nt = NX * NZ * NC
    near = 32
    far = 8
    rows, width = 128, 512
    gated = 256
    half = gated // 2

    def at(dy=0, dx=0, dz=0, dc=0):
        return (
            lax.rem(y + dy, ny), lax.rem(x + dx, NX), lax.rem(z + dz, NZ), lax.rem(c + dc, NC)
        )

    def along(d):
        s = lax.rem(t + (d + nt), nt)
        return (y, s // (NZ * NC), lax.rem(s // NC, NZ), lax.rem(s, NC))

    partner = at(dc=1)
    xs = [at(dx=d) for d in range(1, NX)]
    zs = [at(dz=d) for d in range(1, NZ)]
    ys = [at(dy=d) for d in range(1, ny)]
    yo = [at(dy=d, dc=1) for d in range(ny)]

    link = Links(send, recv, local, partner, spare)
    own, other = pl.ds(0, rows), pl.ds(rows, rows)
    high = pl.ds(near, rows - near)
    low = pl.ds(0, near)
    in_x = link.move(sig.at[0], x0.at[own])
    in_p = link.move(sig.at[0, pl.ds(0, rows - near)], p0.at[high])
    in_w0 = link.move(cw.at[0], w.at[0])
    in_r0 = link.move(rw.at[0], r.at[0])

    barrier = pltpu.get_barrier_semaphore()
    has = {d: (t + d >= 0) & (t + d < nt) for d in (far, -far, 1, -1)}
    greeted = zs + ys + yo + xs

    def greet(device):
        pl.semaphore_signal(barrier, inc=1, device_id=device, device_id_type=MESH)

    for d in (far, -far):
        do_if(has[d], functools.partial(greet, along(d)))
    for device in greeted:
        greet(device)
    count = len(greeted)
    for d in (1, -1):
        do_if(has[d], functools.partial(greet, along(d)))
    for d in (far, -far, 1, -1):
        count = count + has[d].astype(jnp.int32)

    in_go = link.move(go_in.at[0], go.at[own])
    in_sk = link.move(sk_in.at[0], sk.at[own])
    in_r1 = link.move(rw.at[1], r.at[1])
    in_w1 = link.move(cw.at[1], w.at[1])

    def layer0(lo, n):
        part = pl.ds(lo, n)
        zv = mm(p0[part, :], w[0, 0:width, :]) + mm(x0[part, :], w[0, width : 2 * width, :])
        tf = jnp.tanh(zv[:, :gated])
        sg = jax.nn.sigmoid(zv[:, gated:])
        h = (tf * sg).astype(BF)
        tf0[part, :] = tf
        sg0[part, :] = sg
        h0[part, :] = h
        x1[part, :] = (x0[part, :].astype(F32) + mm(h, r[0, :, 0:width])).astype(BF)

    def cleared(ref):
        def clear():
            ref[...] = jnp.zeros(ref.shape, ref.dtype)

        return clear

    do_if(t == 0, cleared(p0.at[low]))
    do_if(t == nt - 1, cleared(dp0r))
    do_if(t >= nt - far, cleared(dpr))
    do_if(t < far, cleared(p1.at[own]))

    in_x.wait()
    in_p.wait()
    in_w0.wait()
    in_r0.wait()
    layer0(near, rows - near)
    in_go.wait()
    in_sk.wait()

    pl.semaphore_wait(barrier, count)
    halo = link.push(x0.at[pl.ds(rows - near, near)], p0.at[low], along(1), has[1], has[-1])
    far_high = link.push(x1.at[high], p1.at[high], along(far), has[far], has[-far])

    in_r1.wait()
    in_w1.wait()
    e1 = mm_t(go[own, :], r[1, :, 0:width]) + mm_t(sk[own, :], r[1, :, width:])
    es0 = mm_t(sk[own, :], r[0, :, width:])

    halo.wait()
    layer0(0, near)
    far_low = link.push(x1.at[low], p1.at[low], along(far), has[far], has[-far])
    first = c == 0
    hk[0, own, :] = jnp.where(first, h0[:, :half], h0[:, half:])
    hs[0] = jnp.where(first, h0[:, half:], h0[:, :half])
    zc1 = mm(x1[own, :], w[1, width : 2 * width, :])

    far_high.wait()
    far_low.wait()
    inputs = (hk.at[0, other, :], go.at[other], sk.at[other])
    rest = (x1.at[other], p1.at[other], x0.at[other], p0.at[other])
    words = sum(math.prod(ref.shape) for ref in inputs + rest)
    shared = Group(link, spare.at[pl.ds(0, words // 256)])
    for src, dst in zip((hs.at[0], go.at[own], sk.at[own]), inputs):
        shared.push(src, dst, partner)
    for ref, dst in zip((x1, p1, x0, p0), rest):
        shared.push(ref.at[own], dst, partner)
    z1 = zc1 + mm(p1[own, :], w[1, 0:width, :])
    tf = jnp.tanh(z1[:, :gated])
    sg = jax.nn.sigmoid(z1[:, gated:])
    h1 = (tf * sg).astype(BF)
    dza = (e1 * sg * (1.0 - tf * tf)).astype(BF)
    dzb = (e1 * tf * sg * (1.0 - sg)).astype(BF)
    dpast = mm_t(dza, w[1, 0:width, 0:gated]) + mm_t(dzb, w[1, 0:width, gated:])
    dp[...] = dpast.astype(BF)
    back = link.push(dp, dpr, along(-far), has[-far], has[far])
    hk[1, own, :] = jnp.where(first, h1[:, :half], h1[:, half:])
    hs[1] = jnp.where(first, h1[:, half:], h1[:, :half])
    h1_there = link.push(hs.at[1], hk.at[1, other, :], partner)
    dz1[own, :] = jnp.where(first, dza, dzb)
    dz1s[...] = jnp.where(first, dzb, dza)
    dz1_there = link.push(dz1s, dz1.at[other], partner)
    wc = mm_t(dza, w[1, width : 2 * width, 0:gated])
    g = go[own, :].astype(F32) + (wc + mm_t(dzb, w[1, width : 2 * width, gated:]))
    gp[...] = g

    def to_x(src, dst):
        group = Group(link, dst)
        for d in range(1, NX):
            group.push(src.at[lax.rem(x + d, NX)], dst.at[d - 1], xs[d - 1])
        return group

    def to_z(src, dst):
        group = Group(link, dst)
        for d in range(1, NZ):
            group.push(src.at[lax.rem(z + d, NZ)], dst.at[d - 1], zs[d - 1])
        return group

    def to_all(src, dst, devices):
        group = Group(link, dst)
        for i, device in enumerate(devices):
            group.push(src, dst.at[i], device)
        return group

    def to_same(ref, i, devices):
        group = Group(link, ref.at[pl.ds(0, len(devices))])
        for device in devices:
            group.push(ref.at[i], ref.at[i], device)
        return group

    def summed(group, own_part, slots):
        group.wait()
        total = own_part.astype(F32)
        for i in range(slots.shape[0]):
            total = total + slots[i].astype(F32)
        return total

    def res_parts(v, buffers):
        parts, slots = buffers[:2]
        cols = v.shape[1] // 2
        for i in range(NX):
            top, left = 64 * (i // 2), cols * (i % 2)
            piece = v[top : top + 64, left : left + cols]
            parts[i] = piece.reshape(8, 8, cols).astype(BF)
        return to_x(parts, slots)

    def res_to_z(copies, buffers):
        parts, slots, out, out_slots = buffers[:4]
        out[...] = summed(copies, parts[x], slots).astype(BF)
        return to_z(out, out_slots)

    def res_direct(v, parts, slots):
        for i in range(NX):
            top, left = 64 * (i // 2), 256 * (i % 2)
            parts[i] = v[top : top + 64, left : left + 256].reshape(8, 8, 256).astype(BF)
        group = Group(link, slots)
        for i in range(1, NX * NZ):
            dx, dz = i // NZ, i % NZ
            src = parts.at[lax.rem(x + dx, NX), lax.rem(z + dz, NZ)]
            group.push(src, slots.at[i - 1], at(dx=dx, dz=dz))
        return group

    def res_to_y(copies, buffers):
        parts, slots, out, out_slots = buffers[2:6]
        out[...] = summed(copies, parts[z], slots).astype(BF)
        return to_all(out, out_slots, ys)

    def res_to_all_z(copies, buffers):
        part, slots, out = buffers[4:7]
        out[z] = (summed(copies, part[...], slots) * factor).astype(BF)
        return to_same(out, z, zs)

    def res_to_all_x(group, buffers):
        part, out, there = buffers[6:9]
        group.wait()
        out[x] = part[...]
        sends = to_same(out, x, xs)
        return sends, link.push(out.at[x], there.at[x], partner, ref=there)

    def res_to_core(state, buffers):
        out, there = buffers[7:9]
        group, sends = state
        group.wait()
        for d in range(1, NX):
            other_x = lax.rem(x + d, NX)
            sends.push(out.at[other_x], there.at[other_x], partner)
        return sends

    def res_pieces(copies, buffers):
        copies.wait()
        for src, core in ((buffers[7], c), (buffers[8], 1 - c)):
            for i in range(NX):
                v = src[i].astype(F32)
                v = v.reshape(64, v.shape[-1]).astype(BF)
                yield pl.ds(pl.multiple_of(core * half + 64 * (i // 2), 64), 64), i % 2, v

    shared.wait()
    h1_there.wait()
    both = [t_mm(hk[1], go[...]), t_mm(hk[1], sk[...]), t_mm(hk[0], sk[...])]
    resa_x = res_parts(jnp.concatenate(both, axis=1), sa)

    def conv_parts(past, cur, dz):
        dzv = dz[...]
        for i in range(NX):
            src = past if i < 2 else cur
            col = (i % 2) * 256
            v = t_mm(src[:, col : col + 256], dzv).reshape(NZ, 2, 16, 256)
            mine0[0][i] = jnp.where(first, v[:, 0], v[:, 1]).astype(BF)
            rest = jnp.where(first, v[:, 1], v[:, 0]).astype(BF)
            left0[0][i] = rest[:, :, :128]
            right0[0][:, i] = rest[:, :, 128:]

    def x_to_z(group, buffers):
        parts, slots, out, out_slots = buffers
        out[...] = summed(group, parts[x], slots).astype(BF)
        return to_z(out, out_slots)

    def z_to_x(group, buffers):
        parts, slots, out, out_slots = buffers
        out[...] = summed(group, parts[z], slots).astype(BF)
        return to_x(out, out_slots)

    def conv_final(layer, copies, part, slots):
        mine = summed(copies[1], part[1], slots.at[1, pl.ds(0, ny - 1)])
        theirs = summed(copies[0], jnp.zeros((16, 256), F32), slots.at[0])
        cgv[layer, :, 0:256] = (jnp.where(first, mine, theirs) * factor).astype(BF)
        cgv[layer, :, 256:512] = (jnp.where(first, theirs, mine) * factor).astype(BF)

    dz1_there.wait()
    dzv = dz1[...]
    for i in range(NX):
        src = p1 if i < 2 else x1
        col = (i % 2) * 256
        v = t_mm(src[:, col : col + 256], dzv).reshape(NZ, 4, 8, 256)
        for k in range(8):
            cs1[k, i] = v[:, k // 2, :, 128 * (k % 2) : 128 * (k % 2) + 128].astype(BF)
    conv1_y = Group(link, cy1)
    for d in range(1, ny):
        conv1_y.push(cs1.at[lax.rem(y + d, ny)], cy1.at[d - 1], ys[d - 1])
    resa_z = res_to_z(resa_x, sa)
    back.wait()
    g1 = gp[...] + dpr[...].astype(F32)
    o0[own, :] = g1.astype(BF)
    o0_there = link.push(o0.at[own], o0.at[other], partner)
    e0 = mm_t(o0[own, :], r[0, :, 0:width]) + es0
    tf = tf0[...]
    sg = sg0[...]
    dza = (e0 * sg * (1.0 - tf * tf)).astype(BF)
    dzb = (e0 * tf * sg * (1.0 - sg)).astype(BF)
    dz0[own, :] = jnp.where(first, dza, dzb)
    dz0s[...] = jnp.where(first, dzb, dza)
    dz0_there = link.push(dz0s, dz0.at[other], partner)
    o0_there.wait()
    resb_x = res_direct(t_mm(hk[0], o0[...]), sb[0], sb[1])
    dz0_there.wait()
    conv_parts(p0, x0, dz0)
    right_z = to_z(right0[0], right0[1])
    mine_x = to_x(mine0[0], mine0[1])
    left_x = to_x(left0[0], left0[1])
    dpast = (mm_t(dza, w[0, 0:width, 0:gated]) + mm_t(dzb, w[0, 0:width, gated:])).astype(BF)
    dp0[...] = dpast
    halo_back = link.push(dp0.at[low], dp0r, along(-1), has[-1], has[1])
    wc = mm_t(dza, w[0, width : 2 * width, 0:gated]) + mm_t(dzb, w[0, width : 2 * width, gated:])
    resa_y = res_to_y(resa_z, sa)
    cx1[...] = summed(conv1_y, cs1[y], cy1).astype(BF)
    conv1_x = to_x(cx1, cxr1)
    mine_z = x_to_z(mine_x, mine0)
    halo_back.wait()
    moved = jnp.concatenate([dp0[near:, :], dp0r[...]], axis=0).astype(F32)
    igv[...] = (g1 + wc + moved).astype(BF)
    link.move(igv, ig_out.at[0], last=True)
    left_z = x_to_z(left_x, left0)
    right_x = z_to_x(right_z, right0)
    sb[4][...] = summed(resb_x, sb[0][x, z], sb[1]).astype(BF)
    resb_y = to_all(sb[4], sb[5], ys)
    cz1[...] = summed(conv1_x, cx1[x], cxr1).astype(BF)
    conv1_z = to_z(cz1, czr1)
    resa_gz = res_to_all_z(resa_y, sa)
    cy0[1] = summed(mine_z, mine0[2][z], mine0[3]).astype(BF)
    mine_y = to_all(cy0.at[1], cyr0.at[1, pl.ds(0, ny - 1)], ys)
    resb_gz = res_to_all_z(resb_y, sb)
    cy0[0, :, 0:128] = summed(left_z, left0[2][z], left0[3]).astype(BF)
    cy0[0, :, 128:256] = summed(right_x, right0[2][x], right0[3]).astype(BF)
    rest_y = to_all(cy0.at[0], cyr0.at[0], yo)
    cg1[c * ny + y] = (summed(conv1_z, cz1[z], czr1) * factor).astype(BF)
    piece = c * ny + y
    conv1_g = to_same(cg1, piece, ys + yo)
    resa_gx = res_to_all_x(resa_gz, sa)
    resb_gx = res_to_all_x(resb_gz, sb)
    conv_final(0, (rest_y, mine_y), cy0, cyr0)
    conv1_g.wait()
    for core in range(NC):
        for k in range(4):
            left = 256 * core + 128 * (k % 2)
            top = 8 * (k // 2)
            cgv[1, top : top + 8, left : left + 128] = cg1[ny * core + 4 * c + k]
    link.move(cgv, cg_out, last=True)
    resa_gc = res_to_core(resa_gx, sa)
    for place, side, v in res_pieces(resa_gc, sa):
        if side:
            rgo[1, place, width:] = v[:, :256]
            rgo[0, place, width:] = v[:, 256:]
        else:
            rgo[1, place, 0:width] = v
    link.move(rgo.at[1], rg_out.at[1], last=True)
    resb_gc = res_to_core(resb_gx, sb)
    for place, side, v in res_pieces(resb_gc, sb):
        rgo[0, place, 256 * side : 256 * side + 256] = v
    link.move(rgo.at[0], rg_out.at[0], last=True)
    link.finish()


def store(*refs):
    n = (len(refs) - 2) // 3
    srcs, dsts, kept = refs[:n], refs[n : 2 * n], refs[2 * n : 3 * n]
    came, went = refs[-2:]
    parts = [(a, i) for a in range(n) for i in range(srcs[a].shape[0])]
    loads = [
        pltpu.make_async_copy(srcs[a].at[i], kept[a].at[i], came.at[k])
        for k, (a, i) in enumerate(parts)
    ]
    stores = [
        pltpu.make_async_copy(kept[a].at[i], dsts[a].at[i], went.at[k])
        for k, (a, i) in enumerate(parts)
    ]
    for load in loads:
        load.start()
    for load, out in zip(loads, stores):
        load.wait()
        out.start()
    for out in stores:
        out.wait()


def body(signal, conv_weight, res_weight, grad_out, skip_cotangent):
    ny = lax.axis_size("dp")
    total = signal.shape[0] * signal.shape[1] * ny * lax.axis_size(TM)
    factor = float(total) ** (-0.5)

    def v(shape, dtype=BF):
        return pltpu.VMEM(shape, dtype)

    def res_scratch(cols, first):
        return [
            v((4, 8, 8, cols)), v((*first, 8, cols)), v((8, 8, cols)), v((7, 8, cols)),
            v((8, cols)), v((ny - 1, 8, cols)), v((8, 8, cols)), v((4, 8, 8, cols)),
            v((4, 8, 8, cols)),
        ]

    remote = 33
    scratch = [
        v((256, 512)), v((256, 512)), v((2, 1024, 512)), v((2, 256, 768)),
        v((256, 512)), v((256, 256)), v((256, 512)), v((256, 512)), v((128, 256)),
        v((128, 256), F32), v((128, 256), F32),
        v((2, 256, 128)), v((2, 128, 128)),
        v((256, 256)), v((128, 256)), v((256, 256)), v((128, 256)),
        v((128, 512), F32), v((256, 512)), v((128, 512)), v((128, 512)), v((128, 512)),
        v((32, 512)), v((128, 512)),
        v((ny, 4, 8, 8, 128)), v((ny - 1, 4, 8, 8, 128)), v((4, 8, 8, 128)), v((3, 8, 8, 128)),
        v((8, 8, 128)), v((7, 8, 128)), v((2 * ny, 8, 128)),
        [v((4, 8, 16, 256)), v((3, 8, 16, 256)), v((8, 16, 256)), v((7, 16, 256))],
        [v((4, 8, 16, 128)), v((3, 8, 16, 128)), v((8, 16, 128)), v((7, 16, 128))],
        [v((8, 4, 16, 128)), v((7, 4, 16, 128)), v((4, 16, 128)), v((3, 16, 128))],
        v((2, 16, 256)), v((2, ny, 16, 256)), v((2, 16, 512)),
        res_scratch(512, (3, 8)), res_scratch(256, (31,)), v((2, 256, 768)), v((8192, 256)),
        pltpu.SemaphoreType.DMA((6,)),
        pltpu.SemaphoreType.DMA((remote,)),
        pltpu.SemaphoreType.DMA((12,)),
    ]
    anyspace = pl.BlockSpec(memory_space=pl.ANY)
    results = pl.pallas_call(
        functools.partial(kernel, ny, factor),
        out_shape=(
            jax.ShapeDtypeStruct((1, 128, 512), BF),
            jax.ShapeDtypeStruct((2, 16, 512), BF),
            jax.ShapeDtypeStruct((2, 256, 768), BF),
        ),
        in_specs=[anyspace] * 5,
        out_specs=(anyspace,) * 3,
        scratch_shapes=scratch,
        compiler_params=pltpu.CompilerParams(collective_id=0, has_side_effects=True),
        name="step",
    )(signal, conv_weight, res_weight, grad_out, skip_cotangent)
    n = sum(a.shape[0] for a in results)
    return pl.pallas_call(
        store,
        out_shape=tuple(jax.ShapeDtypeStruct(a.shape, a.dtype) for a in results),
        in_specs=[anyspace] * 3,
        out_specs=(anyspace,) * 3,
        scratch_shapes=[v(a.shape) for a in results] + [pltpu.SemaphoreType.DMA((n,))] * 2,
        name="store",
    )(*results)


def solution(mesh):
    split = Mesh(mesh.devices.reshape(mesh.shape["dp"], NX, NZ, NC), ("dp", *TM))
    return jax.shard_map(
        body,
        mesh=split,
        in_specs=(P("dp", TM, None), P(), P(), P("dp", TM, None), P("dp", TM, None)),
        out_specs=(P("dp", TM, None), P(None, TM, None), P()),
        check_vma=False,
    )
```
